768 devices in a mesh: seq: 32 (over z_hi, y), chan: 24 (over z_lo, x, core).
Axes of the slice: x: 4, y: 8, z: 12 (z_hi: 4, z_lo: 3; z = z_hi * 3 + z_lo), core: 2. Of those that a mesh axis runs over, the one named last changes fastest.
Arguments:
- query_in: bfloat16 [4096, 6144], P('seq', 'chan'), may hold values from -6 to 6
- key_in: bfloat16 [4096, 6144], P('seq', 'chan'), may hold values from -6 to 6
- value_in: bfloat16 [4096, 6144], P('seq', 'chan'), may hold values from -6 to 6
- filters: bfloat16 [384, 128], P('chan'), may hold values from -0.5 to 0.5
- doc_lengths: int32 [16], replicated, may hold values from 1 to 1024, 4096 in all
- w_out: bfloat16 [6144, 6144], P('chan'), may hold values from -0.125 to 0.125
- cotangent: bfloat16 [4096, 6144], P('seq', 'chan'), may hold values from -6 to 6
Outputs:
- block_out: bfloat16 [4096, 6144], P('seq', 'chan')
- grad_query: bfloat16 [4096, 6144], P('seq', 'chan')
- grad_key: bfloat16 [4096, 6144], P('seq', 'chan')
- grad_value: bfloat16 [4096, 6144], P('seq', 'chan')
- grad_w_out: bfloat16 [6144, 6144], P('chan', 'seq')
- grad_filters: float32 [384, 128], P('chan', 'seq')
The draws below stay inside these ranges and needn't reach their ends.
Inputs may be any that keep to these rules, and one draw needn't show every extreme that they name: `doc_lengths`: the lengths sum to 4096.
All inputs are finite; a program needn't handle non-finite values.
Results may differ from the reference program's by a relative error of at most 0.02.
Values may be sent and summed in bfloat16 or wider, within the bound.
No kernel may reach another device: no remote copies, remote signals or barrier semaphores. Data moves between devices by JAX's collectives and lax.ppermute only.
A program may use at most 32 MiB of HBM per device.

```python
import math
import jax
import jax.numpy as jnp
import numpy as np
from jax import lax

D = 6144
GROUP = 16
LTAP = 128
NDOCS = 16
TOK_DEV = 128
TOKENS = 4096
CH_DEV = 256
NGROUPS = 384
N_SEQ = 32
N_CHAN = 24


def strengthened(drawn, key, source, target, parts, factor):
    owner, partner = [(jnp.arange(drawn.shape[position]) // (drawn.shape[position] // parts)).reshape([-1 if axis == position else 1 for axis in range(drawn.ndim)]) for position in (source, target)]
    chosen = jax.random.permutation(key, parts)[partner]
    strong = (owner == chosen) | (owner == (partner + parts // 2) % parts)
    return jnp.where(strong, factor * drawn, drawn)


def steps_of(key, extent, shards, low, largest):
    def one(position, blocks):
        draws = jax.random.uniform(jax.random.fold_in(jax.random.fold_in(key, 6), position), (blocks,), jnp.float32, low / len(shards), largest / len(shards))
        return jnp.repeat(jnp.exp(draws), extent[position] // blocks).reshape((-1,) + (1,) * (len(extent) - position - 1))

    loudness = one(*shards[0])
    for cut in shards[1:]:
        loudness = loudness * one(*cut)
    return loudness


def length_profile(amount, total, most, lean):
    weights = [(1 << 20) // math.isqrt(rank ** lean) + 1 for rank in range(2, amount + 1)]
    surplus, given = total - most - (amount - 1), [1] * (amount - 1)
    while surplus > 0:
        free = [i for i in range(amount - 1) if given[i] < most]
        mass, remaining = sum([weights[i] for i in free]), surplus
        for i in free:
            addition = min(most - given[i], max(1, remaining * weights[i] // mass), surplus)
            given[i] = given[i] + addition
            surplus = surplus - addition
    return np.array([most] + given)


def ragged_sizes(own_key, number_of, total, limit, slope):
    if number_of == 2:
        one = jax.random.randint(own_key, (), max(1, total - limit), min(limit, total - 1) + 1)
        return jnp.stack([one, total - one])
    tallies = jnp.asarray(length_profile(number_of, total, limit, slope), jnp.int32)
    pairs = (number_of - 1) // 2
    source_of, receiver = tallies[1:1 + 2 * pairs:2], tallies[2:2 + 2 * pairs:2]
    room = jnp.minimum(source_of - 1, limit - receiver)
    moved = jax.random.randint(jax.random.fold_in(own_key, 1), (pairs,), 0, 1 << 20) % (room + 1)
    tallies = tallies.at[1:1 + 2 * pairs:2].set(source_of - moved).at[2:2 + 2 * pairs:2].set(receiver + moved)
    return tallies[jax.random.permutation(jax.random.fold_in(own_key, 2), number_of)]


def bell_draw(stream_key, dims, deviation, reach, pieces=(), kind=jnp.bfloat16):
    gain = steps_of(stream_key, dims, pieces, -0.22, 0.18) if pieces else 1.0
    values = jax.random.normal(stream_key, dims, jnp.float32) * deviation * gain
    return jnp.minimum(jnp.maximum(values, -reach), reach).astype(kind)


def gaussian_with(rng, extent, spread, bound, pieces, heavy, kind=jnp.bfloat16):
    entries = spread * jax.random.normal(rng, extent, jnp.float32)
    if pieces:
        entries = entries * steps_of(rng, extent, pieces, -0.22, 0.18)
    return jnp.clip(strengthened(entries, jax.random.fold_in(rng, 3), *heavy), -bound, bound).astype(kind)


def setup_inputs(seed: int = 0) -> dict:
    key_list = jax.random.split(jax.random.key(seed), 8)
    query_in = bell_draw(key_list[0], (TOKENS, D), 1.0, 6.0, ((0, 32), (1, 24)))
    key_in = bell_draw(key_list[1], (TOKENS, D), 1.0, 6.0, ((0, 32), (1, 24)))
    value_in = bell_draw(key_list[2], (TOKENS, D), 1.0, 6.0, ((0, 32), (1, 24)))
    filters = bell_draw(key_list[3], (NGROUPS, LTAP), LTAP ** -0.5, 0.5, ((0, 24),))
    doc_lengths = ragged_sizes(key_list[4], NDOCS, TOKENS, TOKENS // 4, 2).astype(jnp.int32)
    w_out = gaussian_with(key_list[5], (D, D), D ** -0.5, 0.125, ((0, 24),), (0, 1, 24, 2.25))
    cotangent = gaussian_with(key_list[6], (TOKENS, D), 1.0, 6.0, ((0, 32), (1, 24)), (0, 1, 32, 2.75))
    return dict(query_in=query_in, key_in=key_in, value_in=value_in, filters=filters, doc_lengths=doc_lengths, w_out=w_out, cotangent=cotangent)


def doc_start(positions, starts):
    before = starts[None, :] <= positions[:, None]
    return lax.optimization_barrier(jnp.max(jnp.where(before, starts[None, :], 0), axis=1))

def reference(query_in, key_in, value_in, filters, doc_lengths, w_out, cotangent):
    starts = jnp.cumsum(doc_lengths) - doc_lengths
    positions = jnp.arange(TOKENS, dtype=jnp.int32)
    own_start = doc_start(positions, starts)
    tap_reach = LTAP - 1
    product_kv = lax.optimization_barrier((key_in.astype(jnp.float32) * value_in.astype(jnp.float32)).astype(jnp.bfloat16)).astype(jnp.float32)
    per_channel = jnp.repeat(filters.astype(jnp.float32), GROUP, axis=0)
    mixed_pad = jnp.concatenate([jnp.zeros((tap_reach, D), jnp.float32), product_kv], axis=0)
    tap_ids = jnp.arange(LTAP, dtype=jnp.int32)

    def forward_tap(running, tap):
        source = lax.dynamic_slice_in_dim(mixed_pad, tap_reach - tap, TOKENS, 0)
        keep = (positions - tap >= own_start).astype(jnp.float32)
        weight_col = lax.dynamic_index_in_dim(per_channel, tap, 1, keepdims=False)
        return (running + source * keep[:, None] * weight_col[None, :], None)
    filtered, _ = lax.scan(forward_tap, jnp.zeros((TOKENS, D), jnp.float32), tap_ids)
    gated = (query_in.astype(jnp.float32) * filtered).astype(jnp.bfloat16)

    def out_group(running, index):
        rows_in = lax.dynamic_slice_in_dim(gated, index * CH_DEV, CH_DEV, 1)
        weights = lax.dynamic_slice_in_dim(w_out, index * CH_DEV, CH_DEV, 0)
        term = lax.optimization_barrier(jnp.dot(rows_in, weights, preferred_element_type=jnp.float32).astype(jnp.bfloat16))
        return (running + term.astype(jnp.float32), None)
    out_total, _ = lax.scan(out_group, jnp.zeros((TOKENS, D), jnp.float32), jnp.arange(N_CHAN, dtype=jnp.int32))
    block_out = out_total.astype(jnp.bfloat16)
    grad_in = jnp.dot(cotangent, w_out.T, preferred_element_type=jnp.float32)
    grad_gate = lax.optimization_barrier((grad_in * query_in.astype(jnp.float32)).astype(jnp.bfloat16)).astype(jnp.float32)
    grad_query = (grad_in * filtered).astype(jnp.bfloat16)
    grad_pad = jnp.concatenate([grad_gate, jnp.zeros((tap_reach, D), jnp.float32)], axis=0)

    def back_tap(running, tap):
        source = lax.dynamic_slice_in_dim(grad_pad, tap, TOKENS, 0)
        keep = (positions >= doc_start(positions + tap, starts)).astype(jnp.float32)
        weight_col = lax.dynamic_index_in_dim(per_channel, tap, 1, keepdims=False)
        return (running + source * keep[:, None] * weight_col[None, :], None)
    grad_mixed, _ = lax.scan(back_tap, jnp.zeros((TOKENS, D), jnp.float32), tap_ids)
    grad_key = (grad_mixed * value_in.astype(jnp.float32)).astype(jnp.bfloat16)
    grad_value = (grad_mixed * key_in.astype(jnp.float32)).astype(jnp.bfloat16)

    def tap_grad(running, tap):
        source = lax.dynamic_slice_in_dim(mixed_pad, tap_reach - tap, TOKENS, 0)
        keep = (positions - tap >= own_start).astype(jnp.float32)
        terms = (grad_gate * source * keep[:, None]).reshape(N_SEQ, TOK_DEV, NGROUPS, GROUP).sum(axis=(1, 3))
        shard_terms = lax.optimization_barrier(terms.astype(jnp.bfloat16)).astype(jnp.float32)
        return (running, lax.optimization_barrier(jnp.sum(shard_terms, axis=0)))
    _, per_tap = lax.scan(tap_grad, jnp.zeros((), jnp.float32), tap_ids)
    grad_filters = per_tap.T

    def weight_shard(running, index):
        rows_gated = lax.dynamic_slice_in_dim(gated, index * TOK_DEV, TOK_DEV, 0)
        rows_cot = lax.dynamic_slice_in_dim(cotangent, index * TOK_DEV, TOK_DEV, 0)
        term = lax.optimization_barrier(jnp.dot(rows_gated.T, rows_cot, preferred_element_type=jnp.float32).astype(jnp.bfloat16))
        return (running + term.astype(jnp.float32), None)
    weight_total, _ = lax.scan(weight_shard, jnp.zeros((D, D), jnp.float32), jnp.arange(N_SEQ, dtype=jnp.int32))
    grad_w_out = weight_total.astype(jnp.bfloat16)
    return (block_out, grad_query, grad_key, grad_value, grad_w_out, grad_filters)
```

```python
import jax
import jax.numpy as jnp
from jax import lax
from jax.sharding import Mesh, PartitionSpec as P

SEQ, CHAN = ("zh", "y"), ("zl", "x", "core")


def from_behind(value, axis, steps):
    count = lax.axis_size(axis)
    leading, last = (max(0, -steps), min(count, count - steps))
    return lax.ppermute(value, axis, [(source, source + steps) for source in range(leading, last)])


def doc_start(positions, starts):
    before = starts[None, :] <= positions[:, None]
    return jnp.max(jnp.where(before, starts[None, :], 0), axis=1)


def banded(tap_rows, tok_rows):
    group_count, length = tap_rows.shape
    padded = jnp.concatenate([tap_rows, jnp.zeros((group_count, tok_rows), tap_rows.dtype)], axis=1)
    tiled_taps = jnp.tile(padded, (1, tok_rows))
    return tiled_taps[:, : tok_rows * (tok_rows + length - 1)].reshape(
        group_count, tok_rows, tok_rows + length - 1
    )


def exchange(value, axes):
    return lax.all_to_all(value, axes, 0, 0, tiled=True)


def swap_cores(value):
    return lax.ppermute(value, "core", [(0, 1), (1, 0)])


def gather_rows(cotangent):
    tok_rows, width = cotangent.shape
    chips = lax.axis_size(("zl", "x"))
    mine = exchange(jnp.broadcast_to(cotangent[None], (chips, tok_rows, width)), ("zl", "x"))
    other = swap_cores(mine)
    first = lax.axis_index("core") == 0
    even, odd = jnp.where(first, mine, other), jnp.where(first, other, mine)
    pieces = [piece for pair in zip(even, odd) for piece in pair]
    return jnp.concatenate(pieces, axis=1)


def scatter_sum(partial):
    chips, cores, tok_rows, width = partial.shape
    core = lax.axis_index("core")
    kept = lax.dynamic_index_in_dim(partial, core, 1, keepdims=False)
    sent = lax.dynamic_index_in_dim(partial, 1 - core, 1, keepdims=False)
    pair = (kept + swap_cores(sent.astype(jnp.bfloat16)).astype(jnp.float32)).astype(jnp.bfloat16)
    return jnp.sum(exchange(pair, ("zl", "x")).astype(jnp.float32), axis=0)


def apply_filter(forward_band, mixed_ext, query_in):
    tok_rows, chan_count = query_in.shape
    group_count = forward_band.shape[0]
    grouped = mixed_ext.reshape(mixed_ext.shape[0], group_count, chan_count // group_count)
    filtered = jnp.einsum(
        "gti,igc->tgc", forward_band, grouped, preferred_element_type=jnp.float32
    ).reshape(tok_rows, chan_count)
    gated = (query_in.astype(jnp.float32) * filtered).astype(jnp.bfloat16)
    return (filtered, gated)


def body(query_in, key_in, value_in, filters, doc_lengths, w_out, cotangent):
    tok_rows, chan_count = query_in.shape
    group_count, length = filters.shape
    tap_reach = length - 1
    n_zh, n_y = lax.axis_size("zh"), lax.axis_size("y")
    n_chip = lax.axis_size(("zl", "x"))
    product_kv = (key_in.astype(jnp.float32) * value_in.astype(jnp.float32)).astype(jnp.bfloat16)
    earlier = from_behind(product_kv[tok_rows - tap_reach :], SEQ, 1)
    starts = jnp.cumsum(doc_lengths) - doc_lengths
    first_row = lax.axis_index(SEQ) * tok_rows
    local_steps = jnp.arange(tok_rows, dtype=jnp.int32)
    wide_steps = jnp.arange(tok_rows + tap_reach, dtype=jnp.int32)
    own_pos = first_row + local_steps
    fwd_mask = (first_row - tap_reach + wide_steps)[None, :] >= doc_start(own_pos, starts)[:, None]
    back_mask = own_pos[:, None] >= doc_start(first_row + wide_steps, starts)[None, :]
    forward_band = banded(jnp.flip(filters, 1), tok_rows) * fwd_mask.astype(jnp.bfloat16)[None]
    backward_band = banded(filters, tok_rows) * back_mask.astype(jnp.bfloat16)[None]
    rows = gather_rows(cotangent)
    grad_in = jnp.einsum("tn,cn->tc", rows, w_out, preferred_element_type=jnp.float32)
    grad_gate = (grad_in * query_in.astype(jnp.float32)).astype(jnp.bfloat16)
    later_rows = from_behind(grad_gate[:tap_reach], SEQ, -1)
    mixed_ext = jnp.concatenate([earlier, product_kv], axis=0)
    filtered, gated = apply_filter(forward_band, mixed_ext, query_in)
    grad_query = (grad_in * filtered).astype(jnp.bfloat16)
    w_parts = w_out.reshape(chan_count, n_chip, 2, chan_count)
    partial_out = jnp.einsum("tc,cjkn->jktn", gated, w_parts, preferred_element_type=jnp.float32)
    block_out = scatter_sum(partial_out).astype(jnp.bfloat16)
    grad_ext = jnp.concatenate([grad_gate, later_rows], axis=0)
    per_group = chan_count // group_count
    grad_mixed = jnp.einsum(
        "gtr,rgc->tgc",
        backward_band,
        grad_ext.reshape(tok_rows + tap_reach, group_count, per_group),
        preferred_element_type=jnp.float32,
    ).reshape(tok_rows, chan_count)
    grad_key = (grad_mixed * value_in.astype(jnp.float32)).astype(jnp.bfloat16)
    grad_value = (grad_mixed * key_in.astype(jnp.float32)).astype(jnp.bfloat16)
    pair_terms = jnp.einsum(
        "tgc,igc->gti",
        grad_gate.reshape(tok_rows, group_count, per_group),
        mixed_ext.reshape(tok_rows + tap_reach, group_count, per_group),
        preferred_element_type=jnp.float32,
    )
    pair_terms = pair_terms * fwd_mask.astype(jnp.float32)[None]
    flat_pairs = pair_terms.reshape(group_count, tok_rows * (tok_rows + tap_reach))
    flat_pairs = jnp.concatenate(
        [flat_pairs, jnp.zeros((group_count, tok_rows), jnp.float32)], axis=1
    )
    diagonals = flat_pairs.reshape(group_count, tok_rows, tok_rows + length)[:, :, :length]
    tap_part = jnp.flip(jnp.sum(diagonals, axis=1), 1).astype(jnp.bfloat16)
    owned = length // (n_zh * n_y)
    tap_rows = jnp.transpose(tap_part.reshape(group_count, n_zh, n_y, owned), (2, 1, 0, 3))
    tap_rows = tap_rows.reshape(n_y, n_zh, 1, group_count * owned)
    tap_rows = jnp.pad(tap_rows, ((0, 0), (0, 0), (0, 15), (0, chan_count - group_count * owned)))
    weight_part = jnp.einsum("tn,tc->nc", rows, gated, preferred_element_type=jnp.float32)
    weight_part = weight_part.astype(jnp.bfloat16)
    columns = weight_part.shape[0] // (n_zh * n_y)
    weight_part = jnp.transpose(weight_part.reshape(n_zh, n_y, columns, chan_count), (1, 0, 2, 3))
    terms = jnp.concatenate([weight_part, tap_rows], axis=2)
    over_y = jnp.sum(exchange(terms, "y").reshape(terms.shape).astype(jnp.float32), axis=0)
    over_seq = exchange(over_y.astype(jnp.bfloat16), "zh").astype(jnp.float32)
    total = jnp.sum(over_seq, axis=0)
    weight_sum = total[:columns].T.astype(jnp.bfloat16)
    tap_sum = total[columns, : group_count * owned].reshape(group_count, owned)
    return (block_out, grad_query, grad_key, grad_value, weight_sum, tap_sum)


def build(fine):
    both, rows = P(SEQ, CHAN), P(CHAN, None)
    return jax.shard_map(
        body,
        mesh=fine,
        in_specs=(both, both, both, rows, P(), rows, both),
        out_specs=(both, both, both, both, P(CHAN, SEQ), P(CHAN, SEQ)),
        check_vma=False,
    )


def solution(mesh):
    return build(Mesh(mesh.devices.reshape(4, 8, 3, 4, 2), SEQ + CHAN))
```

```python
import jax
import jax.numpy as jnp
from jax import lax
from jax.experimental import pallas as pl
from jax.experimental.pallas import tpu as pltpu
from jax.sharding import Mesh, PartitionSpec as P

SEQ, CHAN, CHIPS = ("zh", "y"), ("zl", "x", "core"), ("zl", "x")
F32, BF16 = jnp.float32, jnp.bfloat16
SMEM = pl.BlockSpec(memory_space=pltpu.SMEM)
VMEM = pl.BlockSpec(memory_space=pltpu.VMEM)


def iota(shape, axis):
    return lax.broadcasted_iota(jnp.int32, shape, axis)


def start_at(where_ref, count, pos):
    found, running = jnp.zeros(pos.shape, jnp.int32), jnp.int32(0)
    for doc in range(count):
        found = jnp.where(pos >= running, running, found)
        running = running + where_ref[doc]
    return found


def forward_mask(where_ref, docs, rows, flipped=False):
    first = where_ref[docs]
    own = first + (rows - 1 - iota((rows, 2 * rows), 0) if flipped else iota((rows, 2 * rows), 0))
    source = first - rows + iota((rows, 2 * rows), 1)
    return source >= start_at(where_ref, docs, own)


def backward_mask(where_ref, docs, rows):
    first = where_ref[docs]
    start = start_at(where_ref, docs, first + iota((8, 2 * rows), 1))[0:1]
    return first + iota((rows, 2 * rows), 0) >= start


def spread(row, rows):
    return pltpu.roll(jnp.broadcast_to(row, (rows, row.shape[1])), 0, 1, stride=1, stride_axis=0)


def apply_bands(taps_ref, mask, ext, rows, half, per_group):
    member = iota((rows, half), 1) // per_group
    outs = []
    for side in range(ext.shape[1] // half):
        total = jnp.zeros((rows, half), F32)
        piece = ext[:, side * half : (side + 1) * half]
        for group in range(half // per_group):
            index = side * (half // per_group) + group
            band = jnp.where(mask, spread(taps_ref[index : index + 1, :], rows), 0.0).astype(BF16)
            value = jnp.dot(band, piece, preferred_element_type=F32)
            total = jnp.where(member == group, value, total)
        outs.append(total)
    return outs


def filter_kernel(docs, per_group, where_ref, taps_ref, prev_ref, prod_ref, q_ref, filt_ref, gated_ref):
    rows, half = prod_ref.shape[0], 128
    mask = forward_mask(where_ref, docs, rows)
    ext = jnp.concatenate([prev_ref[...], prod_ref[...]], axis=0)
    for side, total in enumerate(apply_bands(taps_ref, mask, ext, rows, half, per_group)):
        lanes = slice(side * half, (side + 1) * half)
        filt_ref[:, lanes] = total
        gated_ref[:, lanes] = (q_ref[:, lanes].astype(F32) * total).astype(BF16)


def grad_kernel(
    docs, per_group, where_ref, mine_ref, other_ref, w_ref, q_ref, filt_ref, gated_ref, prev_ref, prod_ref,
    gate_ref, query_ref, pay_ref, sums,
):
    rows, half = prod_ref.shape[0], 128
    blocks, part, wide = mine_ref.shape
    core = where_ref[docs + 1]
    for ref, at in ((mine_ref, core), (other_ref, 1 - core)):
        total = jnp.zeros((part, w_ref.shape[0]), F32)
        for block in range(blocks):
            total = total + lax.dot_general(
                ref[block], w_ref[:, block * wide : (block + 1) * wide], (((1,), (1,)), ((), ())),
                preferred_element_type=F32,
            )
        sums[pl.ds(pl.multiple_of(at * part, part), part), :] = total
    grad_in = sums[...]
    gate = (grad_in * q_ref[...].astype(F32)).astype(BF16)
    gate_ref[...] = gate
    query_ref[...] = (grad_in * filt_ref[...]).astype(BF16)
    mask = forward_mask(where_ref, docs, rows, True)
    mirror = (iota((rows, rows), 0) + iota((rows, rows), 1) == rows - 1).astype(F32).astype(BF16)
    flipped = jnp.dot(mirror, gate, preferred_element_type=F32)
    member = iota((rows, half), 1) // per_group
    lines = []
    for side in range(prod_ref.shape[1] // half):
        lanes = slice(side * half, (side + 1) * half)
        ext = jnp.concatenate([prev_ref[:, lanes], prod_ref[:, lanes]], axis=0)
        for group in range(half // per_group):
            chosen = jnp.where(member == group, flipped[:, lanes], 0.0).astype(BF16)
            pairs = lax.dot_general(chosen, ext, (((1,), (1,)), ((), ())), preferred_element_type=F32)
            pairs = jnp.where(mask, pairs, 0.0)
            pairs = pltpu.roll(pairs, rows + 1, 1, stride=1, stride_axis=0)
            lines.append(jnp.sum(pairs, axis=0, keepdims=True))
    taps = jnp.concatenate(lines, axis=0).astype(BF16)
    for peer in range(pay_ref.shape[0]):
        pay_ref[peer, :rows, :] = gated_ref[...]
        pay_ref[peer, rows:, :] = taps


def back_kernel(docs, per_group, where_ref, taps_ref, gate_ref, next_ref, k_ref, v_ref, key_ref, value_ref):
    rows, half = gate_ref.shape[0], 128
    mask = backward_mask(where_ref, docs, rows)
    ext = jnp.concatenate([gate_ref[...], next_ref[...]], axis=0)
    for side, total in enumerate(apply_bands(taps_ref, mask, ext, rows, half, per_group)):
        lanes = slice(side * half, (side + 1) * half)
        key_ref[:, lanes] = (total * v_ref[:, lanes].astype(F32)).astype(BF16)
        value_ref[:, lanes] = (total * k_ref[:, lanes].astype(F32)).astype(BF16)


def pick_kernel(unit, columns, rows_ref, out_ref):
    peers, part, wide = out_ref.shape
    block, lanes = rows_ref.shape[2], 128
    per_chunk, chunks = columns // unit, wide // columns
    low = iota((part, lanes), 1) < unit

    def half(index, upper):
        start = index * unit // lanes * lanes
        tile = rows_ref[start // block, :, start % block : start % block + lanes].astype(F32)
        return tile if (index % 2 == 1) == upper else pltpu.roll(tile, unit, 1)

    for peer in range(peers):
        units = [(c * peers + peer) * per_chunk + u for c in range(chunks) for u in range(per_chunk)]
        for tile in range(wide // lanes):
            a, b = units[2 * tile], units[2 * tile + 1]
            out_ref[peer, :, tile * lanes : (tile + 1) * lanes] = jnp.where(low, half(a, False), half(b, True)).astype(BF16)


def project_sent(docs, where_ref, gated_ref, w_ref, out_ref):
    blocks, _, width = out_ref.shape
    core = 1 - where_ref[docs + 1]
    for block in range(blocks):
        lanes = pl.ds(pl.multiple_of((2 * block + core) * width, width), width)
        out_ref[block] = jnp.dot(gated_ref[...], w_ref[:, lanes], preferred_element_type=F32).astype(BF16)


def project_kept(docs, where_ref, gated_ref, w_ref, came_ref, out_ref):
    blocks, _, width = out_ref.shape
    core = where_ref[docs + 1]
    for block in range(blocks):
        lanes = pl.ds(pl.multiple_of((2 * block + core) * width, width), width)
        total = jnp.dot(gated_ref[...], w_ref[:, lanes], preferred_element_type=F32)
        out_ref[block] = (total + came_ref[block].astype(F32)).astype(BF16)


def call(kernel, outs, ins, scratch=(), name=None):
    return pl.pallas_call(
        kernel,
        out_shape=outs,
        in_specs=[SMEM if a.dtype == jnp.int32 else VMEM for a in ins],
        out_specs=jax.tree.map(lambda _: VMEM, outs),
        scratch_shapes=list(scratch),
        name=name,
    )(*ins)


def like(shape, dtype=BF16):
    return jax.ShapeDtypeStruct(shape, dtype)


def shifted(value, axis, steps):
    count = lax.axis_size(axis)
    leading, last = (max(0, -steps), min(count, count - steps))
    return lax.ppermute(value, axis, [(source, source + steps) for source in range(leading, last)])


def exchange(value, axes):
    return lax.all_to_all(value, axes, 0, 0, tiled=True)


def swap_cores(value):
    return lax.ppermute(value, "core", [(0, 1), (1, 0)])


def body(query_in, key_in, value_in, filters, doc_lengths, w_out, cotangent):
    rows, width = query_in.shape
    groups, length = filters.shape
    part, per_group, docs = rows // 2, width // groups, doc_lengths.shape[0]
    n_zh, n_y, n_chip = lax.axis_size("zh"), lax.axis_size("y"), lax.axis_size(CHIPS)
    core, place = lax.axis_index("core"), lax.axis_index(SEQ)
    columns = n_chip * 2 * width // (n_zh * n_y)
    where = jnp.concatenate([doc_lengths, jnp.stack([place * rows, core]).astype(jnp.int32)])

    halves = cotangent.reshape(2, part, width)
    kept = lax.dynamic_index_in_dim(halves, core, 0, keepdims=False)
    came = swap_cores(lax.dynamic_index_in_dim(halves, 1 - core, 0, keepdims=False))
    both = jnp.where(core == 0, jnp.concatenate([kept, came], 1), jnp.concatenate([came, kept], 1))
    mine = exchange(jnp.broadcast_to(both[None], (n_chip, part, 2 * width)), CHIPS)
    picked = call(lambda *r: pick_kernel(64, columns, *r), like((n_y, part, n_zh * columns)), [mine], name="pick")
    picked = exchange(picked, "y")
    other = swap_cores(mine)

    product = (key_in.astype(F32) * value_in.astype(F32)).astype(BF16)
    prev = shifted(product, SEQ, 1)
    taps = filters.astype(F32)
    zeros = jnp.zeros((groups, 2 * rows - length), F32)
    ahead = jnp.concatenate([zeros[:, :1], jnp.flip(taps, 1), zeros[:, 1:]], axis=1)
    behind = jnp.concatenate([taps, zeros], axis=1)
    filtered, gated = call(
        lambda *r: filter_kernel(docs, per_group, *r), (like((rows, width), F32), like((rows, width))),
        [where, ahead, prev, product, query_in], name="filter",
    )
    gate, grad_query, pay = call(
        lambda *r: grad_kernel(docs, per_group, *r),
        (like((rows, width)), like((rows, width)), like((n_y, rows + groups, width))),
        [where, mine, other, w_out, query_in, filtered, gated, prev, product],
        [pltpu.VMEM((rows, width), F32)], name="grad",
    )
    gathered = exchange(pay, "y")
    picked_other = swap_cores(picked)

    sent = call(lambda *r: project_sent(docs, *r), like((n_chip, rows, width)), [where, gated, w_out], name="sent")
    pair = call(
        lambda *r: project_kept(docs, *r), like((n_chip, rows, width)), [where, gated, w_out, swap_cores(sent)], name="kept"
    )
    block_out = jnp.sum(exchange(pair, CHIPS).astype(F32), axis=0).astype(BF16)

    following = shifted(gate, SEQ, -1)
    grad_key, grad_value = call(
        lambda *r: back_kernel(docs, per_group, *r), (like((rows, width)), like((rows, width))),
        [where, behind, gate, following, key_in, value_in], name="back",
    )

    upper, lower = gathered[:, :part], gathered[:, part:rows]
    weight = jnp.einsum("ytn,ytc->nc", picked, jnp.where(core == 0, upper, lower), preferred_element_type=F32)
    weight += jnp.einsum("ytn,ytc->nc", picked_other, jnp.where(core == 0, lower, upper), preferred_element_type=F32)
    tap_terms = jnp.sum(gathered[:, rows:].astype(F32), axis=0).astype(BF16)
    terms = jnp.concatenate(
        [weight.astype(BF16).reshape(n_zh, columns, width), jnp.broadcast_to(tap_terms[None], (n_zh, groups, width))], axis=1
    )
    total = jnp.sum(exchange(terms, "zh").astype(F32), axis=0)
    owned = length // (n_zh * n_y)
    tap_sum = lax.dynamic_slice_in_dim(total[columns:], rows + 1 - (place + 1) * owned, owned, 1)
    return (block_out, grad_query, grad_key, grad_value, total[:columns].T.astype(BF16), jnp.flip(tap_sum, 1))


def build(fine):
    both, rows = P(SEQ, CHAN), P(CHAN, None)
    return jax.shard_map(
        body,
        mesh=fine,
        in_specs=(both, both, both, rows, P(), rows, both),
        out_specs=(both, both, both, both, P(CHAN, SEQ), P(CHAN, SEQ)),
        check_vma=False,
    )


def solution(mesh):
    return build(Mesh(mesh.devices.reshape(4, 8, 3, 4, 2), SEQ + CHAN))
```

```python
import jax
import jax.numpy as jnp
from jax import lax
from jax.experimental import pallas as pl
from jax.experimental.pallas import tpu as pltpu
from jax.sharding import Mesh, PartitionSpec as P

SEQ, CHAN, CHIPS = ("zh", "y"), ("zl", "x", "core"), ("zl", "x")
F32, BF16 = jnp.float32, jnp.bfloat16
TIED = ("pick",)
SMEM = pl.BlockSpec(memory_space=pltpu.SMEM)
VMEM = pl.BlockSpec(memory_space=pltpu.VMEM)


def iota(shape, axis):
    return lax.broadcasted_iota(jnp.int32, shape, axis)


def start_at(where_ref, count, pos):
    found, running = jnp.zeros(pos.shape, jnp.int32), jnp.int32(0)
    for doc in range(count):
        found = jnp.where(pos >= running, running, found)
        running = running + where_ref[doc]
    return found


def forward_mask(where_ref, docs, rows, flipped=False):
    first = where_ref[docs]
    own = first + (rows - 1 - iota((rows, 2 * rows), 0) if flipped else iota((rows, 2 * rows), 0))
    source = first - rows + iota((rows, 2 * rows), 1)
    return source >= start_at(where_ref, docs, own)


def backward_mask(where_ref, docs, rows):
    first = where_ref[docs]
    start = start_at(where_ref, docs, first + iota((8, 2 * rows), 1))[0:1]
    return first + iota((rows, 2 * rows), 0) >= start


def spread(row, rows):
    return pltpu.roll(jnp.broadcast_to(row, (rows, row.shape[1])), 0, 1, stride=1, stride_axis=0)


def apply_bands(taps_ref, mask, ext, rows, half, per_group):
    member = iota((rows, half), 1) // per_group
    outs = []
    for side in range(ext.shape[1] // half):
        total = jnp.zeros((rows, half), F32)
        piece = ext[:, side * half : (side + 1) * half]
        for group in range(half // per_group):
            index = side * (half // per_group) + group
            band = jnp.where(mask, spread(taps_ref[index : index + 1, :], rows), 0.0).astype(BF16)
            value = jnp.dot(band, piece, preferred_element_type=F32)
            total = jnp.where(member == group, value, total)
        outs.append(total)
    return outs


def filter_kernel(docs, per_group, where_ref, taps_ref, prev_ref, prod_ref, q_ref, filt_ref, gated_ref):
    rows, half = prod_ref.shape[0], 128
    mask = forward_mask(where_ref, docs, rows)
    ext = jnp.concatenate([prev_ref[...], prod_ref[...]], axis=0)
    for side, total in enumerate(apply_bands(taps_ref, mask, ext, rows, half, per_group)):
        lanes = slice(side * half, (side + 1) * half)
        filt_ref[:, lanes] = total
        gated_ref[:, lanes] = (q_ref[:, lanes].astype(F32) * total).astype(BF16)


def grad_kernel(
    docs, per_group, where_ref, mine_ref, other_ref, w_ref, q_ref, filt_ref, gated_ref, prev_ref, prod_ref,
    gate_ref, query_ref, pay_ref, sums,
):
    rows, half = prod_ref.shape[0], 128
    blocks, part, wide = mine_ref.shape
    core = where_ref[docs + 1]
    for ref, at in ((mine_ref, core), (other_ref, 1 - core)):
        total = jnp.zeros((part, w_ref.shape[0]), F32)
        for block in range(blocks):
            total = total + lax.dot_general(
                ref[block], w_ref[:, block * wide : (block + 1) * wide], (((1,), (1,)), ((), ())),
                preferred_element_type=F32,
            )
        sums[pl.ds(pl.multiple_of(at * part, part), part), :] = total
    grad_in = sums[...]
    gate = (grad_in * q_ref[...].astype(F32)).astype(BF16)
    gate_ref[...] = gate
    query_ref[...] = (grad_in * filt_ref[...]).astype(BF16)
    mask = forward_mask(where_ref, docs, rows, True)
    mirror = (iota((rows, rows), 0) + iota((rows, rows), 1) == rows - 1).astype(F32).astype(BF16)
    flipped = jnp.dot(mirror, gate, preferred_element_type=F32)
    member = iota((rows, half), 1) // per_group
    lines = []
    for side in range(prod_ref.shape[1] // half):
        lanes = slice(side * half, (side + 1) * half)
        ext = jnp.concatenate([prev_ref[:, lanes], prod_ref[:, lanes]], axis=0)
        for group in range(half // per_group):
            chosen = jnp.where(member == group, flipped[:, lanes], 0.0).astype(BF16)
            pairs = lax.dot_general(chosen, ext, (((1,), (1,)), ((), ())), preferred_element_type=F32)
            pairs = jnp.where(mask, pairs, 0.0)
            pairs = pltpu.roll(pairs, rows + 1, 1, stride=1, stride_axis=0)
            lines.append(jnp.sum(pairs, axis=0, keepdims=True))
    taps = jnp.concatenate(lines, axis=0).astype(BF16)
    for peer in range(pay_ref.shape[0]):
        pay_ref[peer, :rows, :] = gated_ref[...]
        pay_ref[peer, rows:, :] = taps


def back_kernel(docs, per_group, where_ref, taps_ref, gate_ref, next_ref, k_ref, v_ref, key_ref, value_ref):
    rows, half = gate_ref.shape[0], 128
    mask = backward_mask(where_ref, docs, rows)
    ext = jnp.concatenate([gate_ref[...], next_ref[...]], axis=0)
    for side, total in enumerate(apply_bands(taps_ref, mask, ext, rows, half, per_group)):
        lanes = slice(side * half, (side + 1) * half)
        key_ref[:, lanes] = (total * v_ref[:, lanes].astype(F32)).astype(BF16)
        value_ref[:, lanes] = (total * k_ref[:, lanes].astype(F32)).astype(BF16)


def pick_kernel(unit, columns, rows_ref, out_ref):
    peers, part, wide = out_ref.shape
    block, lanes = rows_ref.shape[2], 128
    per_chunk, chunks = columns // unit, wide // columns
    low = iota((part, lanes), 1) < unit

    def half(index, upper):
        start = index * unit // lanes * lanes
        tile = rows_ref[start // block, :, start % block : start % block + lanes].astype(F32)
        return tile if (index % 2 == 1) == upper else pltpu.roll(tile, unit, 1)

    for peer in range(peers):
        units = [(c * peers + peer) * per_chunk + u for c in range(chunks) for u in range(per_chunk)]
        for tile in range(wide // lanes):
            a, b = units[2 * tile], units[2 * tile + 1]
            out_ref[peer, :, tile * lanes : (tile + 1) * lanes] = jnp.where(low, half(a, False), half(b, True)).astype(BF16)


def columns_to(docs, where_ref, n_zl, n_x, step, core, width):
    zl = lax.rem(where_ref[docs + 2] + step // n_x, n_zl)
    x = lax.rem(where_ref[docs + 3] + step % n_x, n_x)
    return pl.ds(pl.multiple_of(((zl * n_x + x) * 2 + core) * width, width), width)


def project_sent(docs, n_zl, n_x, where_ref, gated_ref, w_ref, out_ref):
    blocks, _, width = out_ref.shape
    core = 1 - where_ref[docs + 1]
    for step in range(blocks):
        lanes = columns_to(docs, where_ref, n_zl, n_x, step, core, width)
        out_ref[step] = jnp.dot(gated_ref[...], w_ref[:, lanes], preferred_element_type=F32).astype(BF16)


def project_kept(docs, n_zl, n_x, where_ref, gated_ref, w_ref, came_ref, *out_refs):
    blocks, _, width = came_ref.shape
    core = where_ref[docs + 1]
    for step in range(blocks):
        lanes = columns_to(docs, where_ref, n_zl, n_x, step, core, width)
        total = jnp.dot(gated_ref[...], w_ref[:, lanes], preferred_element_type=F32)
        out_refs[step // n_x][step % n_x] = (total + came_ref[step].astype(F32)).astype(BF16)


def call(kernel, outs, ins, scratch=(), name=None):
    ins = [a if a.dtype == jnp.int32 or name not in TIED else pltpu.with_memory_space_constraint(a, pltpu.VMEM) for a in ins]
    return pl.pallas_call(
        kernel,
        out_shape=outs,
        in_specs=[SMEM if a.dtype == jnp.int32 else VMEM for a in ins],
        out_specs=jax.tree.map(lambda _: VMEM, outs),
        scratch_shapes=list(scratch),
        name=name,
        compiler_params=pltpu.CompilerParams(vmem_limit_bytes=16 << 20),
    )(*ins)


def like(shape, dtype=BF16):
    return jax.ShapeDtypeStruct(shape, dtype)


def shifted(value, axis, steps):
    count = lax.axis_size(axis)
    leading, last = (max(0, -steps), min(count, count - steps))
    return lax.ppermute(value, axis, [(source, source + steps) for source in range(leading, last)])


def exchange(value, axes):
    return lax.all_to_all(value, axes, 0, 0, tiled=True)


def turned(value, axis, steps):
    count = lax.axis_size(axis)
    return lax.ppermute(value, axis, [(source, (source + steps) % count) for source in range(count)])


def swap_cores(value):
    return lax.ppermute(value, "core", [(0, 1), (1, 0)])


def body(query_in, key_in, value_in, filters, doc_lengths, w_out, cotangent):
    rows, width = query_in.shape
    groups, length = filters.shape
    part, per_group, docs = rows // 2, width // groups, doc_lengths.shape[0]
    n_zh, n_y, n_zl, n_x = (lax.axis_size(a) for a in ("zh", "y", "zl", "x"))
    n_chip = n_zl * n_x
    core, place = lax.axis_index("core"), lax.axis_index(SEQ)
    columns = n_chip * 2 * width // (n_zh * n_y)
    spots = jnp.stack([place * rows, core, lax.axis_index("zl"), lax.axis_index("x")])
    where = jnp.concatenate([doc_lengths, spots.astype(jnp.int32)])

    halves = jnp.broadcast_to(cotangent.reshape(1, 2, part, width), (n_chip, 2, part, width))
    mine = exchange(halves.reshape(2 * n_chip, part, width), CHAN)

    product = (key_in.astype(F32) * value_in.astype(F32)).astype(BF16)
    prev = shifted(product, SEQ, 1)
    taps = filters.astype(F32)
    zeros = jnp.zeros((groups, 2 * rows - length), F32)
    ahead = jnp.concatenate([zeros[:, :1], jnp.flip(taps, 1), zeros[:, 1:]], axis=1)
    behind = jnp.concatenate([taps, zeros], axis=1)
    filtered, gated = call(
        lambda *r: filter_kernel(docs, per_group, *r), (like((rows, width), F32), like((rows, width))),
        [where, ahead, prev, product, query_in], name="filter",
    )
    sent = call(
        lambda *r: project_sent(docs, n_zl, n_x, *r), like((n_chip, rows, width)), [where, gated, w_out], name="sent"
    )
    mine, sent = lax.optimization_barrier((mine, sent))
    picked = call(lambda *r: pick_kernel(64, columns, *r), like((n_y, part, n_zh * columns)), [mine], name="pick")
    picked = exchange(picked, "y")
    other, came = swap_cores(mine), swap_cores(sent)
    parts = call(
        lambda *r: project_kept(docs, n_zl, n_x, *r), (like((n_x, rows, width)),) * n_zl,
        [where, gated, w_out, came], name="kept",
    )
    gate, grad_query, pay = call(
        lambda *r: grad_kernel(docs, per_group, *r),
        (like((rows, width)), like((rows, width)), like((n_y, rows + groups, width))),
        [where, mine, other, w_out, query_in, filtered, gated, prev, product],
        [pltpu.VMEM((rows, width), F32)], name="grad",
    )
    pay, parts = lax.optimization_barrier((pay, parts))
    gathered = exchange(pay, "y")
    picked_other = swap_cores(picked)
    following = shifted(gate, SEQ, -1)
    grad_key, grad_value = call(
        lambda *r: back_kernel(docs, per_group, *r), (like((rows, width)), like((rows, width))),
        [where, behind, gate, following, key_in, value_in], name="back",
    )
    along_z = sum((turned(parts[k], "zl", k).astype(F32) for k in range(1, n_zl)), parts[0].astype(F32)).astype(BF16)
    gathered, grad_key, grad_value, along_z = lax.optimization_barrier((gathered, grad_key, grad_value, along_z))
    block_out = sum((turned(along_z[k], "x", k).astype(F32) for k in range(1, n_x)), along_z[0].astype(F32)).astype(BF16)

    upper, lower = gathered[:, :part], gathered[:, part:rows]
    weight = jnp.einsum("ytn,ytc->nc", picked, jnp.where(core == 0, upper, lower), preferred_element_type=F32)
    weight += jnp.einsum("ytn,ytc->nc", picked_other, jnp.where(core == 0, lower, upper), preferred_element_type=F32)
    tap_terms = jnp.sum(gathered[:, rows:].astype(F32), axis=0).astype(BF16)
    terms = jnp.concatenate(
        [weight.astype(BF16).reshape(n_zh, columns, width), jnp.broadcast_to(tap_terms[None], (n_zh, groups, width))], axis=1
    )
    total = jnp.sum(exchange(terms, "zh").astype(F32), axis=0)
    owned = length // (n_zh * n_y)
    tap_sum = lax.dynamic_slice_in_dim(total[columns:], rows + 1 - (place + 1) * owned, owned, 1)
    return (block_out, grad_query, grad_key, grad_value, total[:columns].T.astype(BF16), jnp.flip(tap_sum, 1))


def build(fine):
    both, rows = P(SEQ, CHAN), P(CHAN, None)
    return jax.shard_map(
        body,
        mesh=fine,
        in_specs=(both, both, both, rows, P(), rows, both),
        out_specs=(both, both, both, both, P(CHAN, SEQ), P(CHAN, SEQ)),
        check_vma=False,
    )


def solution(mesh):
    return build(Mesh(mesh.devices.reshape(4, 8, 3, 4, 2), SEQ + CHAN))
```

```python
import jax
import jax.numpy as jnp
from jax import lax
from jax.experimental import pallas as pl
from jax.experimental.pallas import tpu as pltpu
from jax.sharding import Mesh, PartitionSpec as P

SEQ, CHAN = ("zh", "y"), ("zl", "x", "core")
F32, BF16 = jnp.float32, jnp.bfloat16
TIED = ("pick",)
LIMITS = {"entry": None}
SMEM = pl.BlockSpec(memory_space=pltpu.SMEM)
VMEM = pl.BlockSpec(memory_space=pltpu.VMEM)


def iota(shape, axis):
    return lax.broadcasted_iota(jnp.int32, shape, axis)


def start_at(where_ref, count, pos):
    found, running = jnp.zeros(pos.shape, jnp.int32), jnp.int32(0)
    for doc in range(count):
        found = jnp.where(pos >= running, running, found)
        running = running + where_ref[doc]
    return found


def forward_mask(where_ref, docs, rows, flipped=False):
    first = where_ref[docs]
    own = first + (rows - 1 - iota((rows, 2 * rows), 0) if flipped else iota((rows, 2 * rows), 0))
    source = first - rows + iota((rows, 2 * rows), 1)
    return source >= start_at(where_ref, docs, own)


def backward_mask(where_ref, docs, rows):
    first = where_ref[docs]
    start = start_at(where_ref, docs, first + iota((8, 2 * rows), 1))[0:1]
    return first + iota((rows, 2 * rows), 0) >= start


def spread(row, rows):
    return pltpu.roll(jnp.broadcast_to(row, (rows, row.shape[1])), 0, 1, stride=1, stride_axis=0)


def apply_bands(taps_ref, mask, ext, rows, half, per_group):
    member = iota((rows, half), 1) // per_group
    outs = []
    for side in range(ext.shape[1] // half):
        total = jnp.zeros((rows, half), F32)
        piece = ext[:, side * half : (side + 1) * half]
        for group in range(half // per_group):
            index = side * (half // per_group) + group
            band = jnp.where(mask, spread(taps_ref[index : index + 1, :], rows), 0.0).astype(BF16)
            value = jnp.dot(band, piece, preferred_element_type=F32)
            total = jnp.where(member == group, value, total)
        outs.append(total)
    return outs


def entry_kernel(cot_ref, k_ref, v_ref, fan_ref, prod_ref):
    part = fan_ref.shape[1]
    for peer in range(fan_ref.shape[0]):
        fan_ref[peer] = cot_ref[peer % 2 * part : (peer % 2 + 1) * part, :]
    prod_ref[...] = (k_ref[...].astype(F32) * v_ref[...].astype(F32)).astype(BF16)


def filter_kernel(docs, per_group, where_ref, taps_ref, prev_ref, prod_ref, q_ref, filt_ref, gated_ref):
    rows, half = prod_ref.shape[0], 128
    mask = forward_mask(where_ref, docs, rows)
    ext = jnp.concatenate([prev_ref[...], prod_ref[...]], axis=0)
    for side, total in enumerate(apply_bands(taps_ref, mask, ext, rows, half, per_group)):
        lanes = slice(side * half, (side + 1) * half)
        filt_ref[:, lanes] = total
        gated_ref[:, lanes] = (q_ref[:, lanes].astype(F32) * total).astype(BF16)


def grad_kernel(
    docs, per_group, where_ref, mine_ref, other_ref, w_ref, q_ref, filt_ref, gated_ref, prev_ref, prod_ref,
    gate_ref, query_ref, pay_ref, sums,
):
    rows, half = prod_ref.shape[0], 128
    blocks, part, wide = mine_ref.shape
    core = where_ref[docs + 1]
    for ref, at in ((mine_ref, core), (other_ref, 1 - core)):
        total = jnp.zeros((part, w_ref.shape[0]), F32)
        for block in range(blocks):
            total = total + lax.dot_general(
                ref[block], w_ref[:, block * wide : (block + 1) * wide], (((1,), (1,)), ((), ())),
                preferred_element_type=F32,
            )
        sums[pl.ds(pl.multiple_of(at * part, part), part), :] = total
    grad_in = sums[...]
    gate = (grad_in * q_ref[...].astype(F32)).astype(BF16)
    gate_ref[...] = gate
    query_ref[...] = (grad_in * filt_ref[...]).astype(BF16)
    mask = forward_mask(where_ref, docs, rows, True)
    mirror = (iota((rows, rows), 0) + iota((rows, rows), 1) == rows - 1).astype(F32).astype(BF16)
    flipped = jnp.dot(mirror, gate, preferred_element_type=F32)
    member = iota((rows, half), 1) // per_group
    lines = []
    for side in range(prod_ref.shape[1] // half):
        lanes = slice(side * half, (side + 1) * half)
        ext = jnp.concatenate([prev_ref[:, lanes], prod_ref[:, lanes]], axis=0)
        for group in range(half // per_group):
            chosen = jnp.where(member == group, flipped[:, lanes], 0.0).astype(BF16)
            pairs = lax.dot_general(chosen, ext, (((1,), (1,)), ((), ())), preferred_element_type=F32)
            pairs = jnp.where(mask, pairs, 0.0)
            pairs = pltpu.roll(pairs, rows + 1, 1, stride=1, stride_axis=0)
            lines.append(jnp.sum(pairs, axis=0, keepdims=True))
    taps = jnp.concatenate(lines, axis=0).astype(BF16)
    for peer in range(pay_ref.shape[0]):
        pay_ref[peer, :rows, :] = gated_ref[...]
        pay_ref[peer, rows:, :] = taps


def back_kernel(docs, per_group, where_ref, taps_ref, gate_ref, next_ref, k_ref, v_ref, key_ref, value_ref):
    rows, half = gate_ref.shape[0], 128
    mask = backward_mask(where_ref, docs, rows)
    ext = jnp.concatenate([gate_ref[...], next_ref[...]], axis=0)
    for side, total in enumerate(apply_bands(taps_ref, mask, ext, rows, half, per_group)):
        lanes = slice(side * half, (side + 1) * half)
        key_ref[:, lanes] = (total * v_ref[:, lanes].astype(F32)).astype(BF16)
        value_ref[:, lanes] = (total * k_ref[:, lanes].astype(F32)).astype(BF16)


def pick_kernel(unit, columns, rows_ref, out_ref):
    peers, part, wide = out_ref.shape
    block, lanes = rows_ref.shape[2], 128
    per_chunk, chunks = columns // unit, wide // columns
    low = iota((part, lanes), 1) < unit

    def half(index, upper):
        start = index * unit // lanes * lanes
        tile = rows_ref[start // block, :, start % block : start % block + lanes].astype(F32)
        return tile if (index % 2 == 1) == upper else pltpu.roll(tile, unit, 1)

    for peer in range(peers):
        units = [(c * peers + peer) * per_chunk + u for c in range(chunks) for u in range(per_chunk)]
        for tile in range(wide // lanes):
            a, b = units[2 * tile], units[2 * tile + 1]
            out_ref[peer, :, tile * lanes : (tile + 1) * lanes] = jnp.where(low, half(a, False), half(b, True)).astype(BF16)


def columns_to(docs, where_ref, n_zl, n_x, step, core, width):
    zl = lax.rem(where_ref[docs + 2] + step // n_x, n_zl)
    x = lax.rem(where_ref[docs + 3] + step % n_x, n_x)
    return pl.ds(pl.multiple_of(((zl * n_x + x) * 2 + core) * width, width), width)


def project_sent(docs, n_zl, n_x, where_ref, gated_ref, w_ref, out_ref):
    blocks, _, width = out_ref.shape
    core = 1 - where_ref[docs + 1]
    for step in range(blocks):
        lanes = columns_to(docs, where_ref, n_zl, n_x, step, core, width)
        out_ref[step] = jnp.dot(gated_ref[...], w_ref[:, lanes], preferred_element_type=F32).astype(BF16)


def project_kept(docs, n_zl, n_x, where_ref, gated_ref, w_ref, came_ref, *out_refs):
    blocks, _, width = came_ref.shape
    core = where_ref[docs + 1]
    for step in range(blocks):
        lanes = columns_to(docs, where_ref, n_zl, n_x, step, core, width)
        total = jnp.dot(gated_ref[...], w_ref[:, lanes], preferred_element_type=F32)
        out_refs[step // n_x][step % n_x] = (total + came_ref[step].astype(F32)).astype(BF16)


def call(kernel, outs, ins, scratch=(), name=None):
    ins = [a if a.dtype == jnp.int32 or name not in TIED else pltpu.with_memory_space_constraint(a, pltpu.VMEM) for a in ins]
    return pl.pallas_call(
        kernel,
        out_shape=outs,
        in_specs=[SMEM if a.dtype == jnp.int32 else VMEM for a in ins],
        out_specs=jax.tree.map(lambda _: VMEM, outs),
        scratch_shapes=list(scratch),
        compiler_params=pltpu.CompilerParams(vmem_limit_bytes=LIMITS.get(name, 16 << 20)),
    )(*ins)


def like(shape, dtype=BF16):
    return jax.ShapeDtypeStruct(shape, dtype)


def shifted(value, axis, steps):
    count = lax.axis_size(axis)
    leading, last = (max(0, -steps), min(count, count - steps))
    return lax.ppermute(value, axis, [(source, source + steps) for source in range(leading, last)])


def exchange(value, axes):
    return lax.all_to_all(value, axes, 0, 0, tiled=True)


def turned(value, axis, steps):
    count = lax.axis_size(axis)
    return lax.ppermute(value, axis, [(source, (source + steps) % count) for source in range(count)])


def swap_cores(value):
    return lax.ppermute(value, "core", [(0, 1), (1, 0)])


def block(query_in, key_in, value_in, filters, doc_lengths, w_out, cotangent):
    rows, width = query_in.shape
    groups, length = filters.shape
    part, per_group, docs = rows // 2, width // groups, doc_lengths.shape[0]
    n_zh, n_y, n_zl, n_x = (lax.axis_size(a) for a in ("zh", "y", "zl", "x"))
    n_chip = n_zl * n_x
    core, place = lax.axis_index("core"), lax.axis_index(SEQ)
    columns = n_chip * 2 * width // (n_zh * n_y)
    spots = jnp.stack([place * rows, core, lax.axis_index("zl"), lax.axis_index("x")])
    where = jnp.concatenate([doc_lengths, spots.astype(jnp.int32)])

    fan, product = call(
        entry_kernel, (like((2 * n_chip, part, width)), like((rows, width))), [cotangent, key_in, value_in], name="entry"
    )
    mine = exchange(fan, CHAN)
    prev = shifted(product, SEQ, 1)
    taps = filters.astype(F32)
    zeros = jnp.zeros((groups, 2 * rows - length), F32)
    ahead = jnp.concatenate([zeros[:, :1], jnp.flip(taps, 1), zeros[:, 1:]], axis=1)
    behind = jnp.concatenate([taps, zeros], axis=1)
    filtered, gated = call(
        lambda *r: filter_kernel(docs, per_group, *r), (like((rows, width), F32), like((rows, width))),
        [where, ahead, prev, product, query_in], name="filter",
    )
    sent = call(
        lambda *r: project_sent(docs, n_zl, n_x, *r), like((n_chip, rows, width)), [where, gated, w_out], name="sent"
    )
    mine, gated = lax.optimization_barrier((mine, gated))
    picked = call(lambda *r: pick_kernel(64, columns, *r), like((n_y, part, n_zh * columns)), [mine], name="pick")
    picked = exchange(picked, "y")
    other, came = swap_cores(mine), swap_cores(sent)
    parts = call(
        lambda *r: project_kept(docs, n_zl, n_x, *r), (like((n_x, rows, width)),) * n_zl,
        [where, gated, w_out, came], name="kept",
    )
    gate, grad_query, pay = call(
        lambda *r: grad_kernel(docs, per_group, *r),
        (like((rows, width)), like((rows, width)), like((n_y, rows + groups, width))),
        [where, mine, other, w_out, query_in, filtered, gated, prev, product],
        [pltpu.VMEM((rows, width), F32)], name="grad",
    )
    gathered = exchange(pay, "y")
    picked_other = swap_cores(picked)
    following = shifted(gate, SEQ, -1)
    grad_key, grad_value = call(
        lambda *r: back_kernel(docs, per_group, *r), (like((rows, width)), like((rows, width))),
        [where, behind, gate, following, key_in, value_in], name="back",
    )
    along_z = sum((turned(parts[k], "zl", k).astype(F32) for k in range(1, n_zl)), parts[0].astype(F32)).astype(BF16)
    gathered, grad_key, grad_value, along_z = lax.optimization_barrier((gathered, grad_key, grad_value, along_z))
    block_out = sum((turned(along_z[k], "x", k).astype(F32) for k in range(1, n_x)), along_z[0].astype(F32)).astype(BF16)

    upper, lower = gathered[:, :part], gathered[:, part:rows]
    weight = jnp.einsum("ytn,ytc->nc", picked, jnp.where(core == 0, upper, lower), preferred_element_type=F32)
    weight += jnp.einsum("ytn,ytc->nc", picked_other, jnp.where(core == 0, lower, upper), preferred_element_type=F32)
    tap_terms = jnp.sum(gathered[:, rows:].astype(F32), axis=0).astype(BF16)
    terms = jnp.concatenate(
        [weight.astype(BF16).reshape(n_zh, columns, width), jnp.broadcast_to(tap_terms[None], (n_zh, groups, width))], axis=1
    )
    total = jnp.sum(exchange(terms, "zh").astype(F32), axis=0)
    owned = length // (n_zh * n_y)
    tap_sum = lax.dynamic_slice_in_dim(total[columns:], rows + 1 - (place + 1) * owned, owned, 1)
    return (block_out, grad_query, grad_key, grad_value, total[:columns].T.astype(BF16), jnp.flip(tap_sum, 1))


def build(fine):
    both, rows = P(SEQ, CHAN), P(CHAN, None)
    return jax.shard_map(
        block,
        mesh=fine,
        in_specs=(both, both, both, rows, P(), rows, both),
        out_specs=(both, both, both, both, P(CHAN, SEQ), P(CHAN, SEQ)),
        check_vma=False,
    )


def solution(mesh):
    fine = Mesh(mesh.devices.reshape(4, 8, 3, 4, 2), SEQ + CHAN)
    return build(fine)
```

```python
import jax
import jax.numpy as jnp
from jax import lax
from jax.experimental import pallas as pl
from jax.experimental.pallas import tpu as pltpu
from jax.sharding import Mesh, PartitionSpec as P

SEQ, CHAN = ("zh", "y"), ("zl", "x", "core")
F32, BF16 = jnp.float32, jnp.bfloat16
TIED = ("pick",)
LIMITS = {"entry": None}
SMEM = pl.BlockSpec(memory_space=pltpu.SMEM)
VMEM = pl.BlockSpec(memory_space=pltpu.VMEM)


def iota(shape, axis):
    return lax.broadcasted_iota(jnp.int32, shape, axis)


def start_at(where_ref, count, pos):
    found, running = jnp.zeros(pos.shape, jnp.int32), jnp.int32(0)
    for doc in range(count):
        found = jnp.where(pos >= running, running, found)
        running = running + where_ref[doc]
    return found


def forward_mask(where_ref, docs, rows, flipped=False):
    first = where_ref[docs]
    own = first + (rows - 1 - iota((rows, 2 * rows), 0) if flipped else iota((rows, 2 * rows), 0))
    source = first - rows + iota((rows, 2 * rows), 1)
    return source >= start_at(where_ref, docs, own)


def backward_mask(where_ref, docs, rows):
    first = where_ref[docs]
    start = start_at(where_ref, docs, first + iota((8, 2 * rows), 1))[0:1]
    return first + iota((rows, 2 * rows), 0) >= start


def spread(row, rows):
    return pltpu.roll(jnp.broadcast_to(row, (rows, row.shape[1])), 0, 1, stride=1, stride_axis=0)


def apply_bands(taps_ref, mask, ext, rows, half, per_group):
    member = iota((rows, half), 1) // per_group
    outs = []
    for side in range(ext.shape[1] // half):
        total = jnp.zeros((rows, half), F32)
        piece = ext[:, side * half : (side + 1) * half]
        for group in range(half // per_group):
            index = side * (half // per_group) + group
            band = jnp.where(mask, spread(taps_ref[index : index + 1, :], rows), 0.0).astype(BF16)
            value = jnp.dot(band, piece, preferred_element_type=F32)
            total = jnp.where(member == group, value, total)
        outs.append(total)
    return outs


def entry_kernel(cot_ref, k_ref, v_ref, fan_ref, prod_ref):
    part = fan_ref.shape[1]
    for peer in range(fan_ref.shape[0]):
        fan_ref[peer] = cot_ref[peer % 2 * part : (peer % 2 + 1) * part, :]
    prod_ref[...] = (k_ref[...].astype(F32) * v_ref[...].astype(F32)).astype(BF16)


def filter_kernel(docs, per_group, where_ref, taps_ref, prev_ref, prod_ref, q_ref, filt_ref, gated_ref):
    rows, half = prod_ref.shape[0], 128
    mask = forward_mask(where_ref, docs, rows)
    ext = jnp.concatenate([prev_ref[...], prod_ref[...]], axis=0)
    for side, total in enumerate(apply_bands(taps_ref, mask, ext, rows, half, per_group)):
        lanes = slice(side * half, (side + 1) * half)
        filt_ref[:, lanes] = total
        gated_ref[:, lanes] = (q_ref[:, lanes].astype(F32) * total).astype(BF16)


def grad_kernel(
    docs, per_group, where_ref, mine_ref, other_ref, w_ref, q_ref, filt_ref, gated_ref, prev_ref, prod_ref,
    gate_ref, query_ref, pay_ref, sums,
):
    rows, half = prod_ref.shape[0], 128
    blocks, part, wide = mine_ref.shape
    core = where_ref[docs + 1]
    for ref, at in ((mine_ref, core), (other_ref, 1 - core)):
        total = jnp.zeros((part, w_ref.shape[0]), F32)
        for block in range(blocks):
            total = total + lax.dot_general(
                ref[block], w_ref[:, block * wide : (block + 1) * wide], (((1,), (1,)), ((), ())),
                preferred_element_type=F32,
            )
        sums[pl.ds(pl.multiple_of(at * part, part), part), :] = total
    grad_in = sums[...]
    gate = (grad_in * q_ref[...].astype(F32)).astype(BF16)
    gate_ref[...] = gate
    query_ref[...] = (grad_in * filt_ref[...]).astype(BF16)
    mask = forward_mask(where_ref, docs, rows, True)
    mirror = (iota((rows, rows), 0) + iota((rows, rows), 1) == rows - 1).astype(F32).astype(BF16)
    flipped = jnp.dot(mirror, gate, preferred_element_type=F32)
    member = iota((rows, half), 1) // per_group
    lines = []
    for side in range(prod_ref.shape[1] // half):
        lanes = slice(side * half, (side + 1) * half)
        ext = jnp.concatenate([prev_ref[:, lanes], prod_ref[:, lanes]], axis=0)
        for group in range(half // per_group):
            chosen = jnp.where(member == group, flipped[:, lanes], 0.0).astype(BF16)
            pairs = lax.dot_general(chosen, ext, (((1,), (1,)), ((), ())), preferred_element_type=F32)
            pairs = jnp.where(mask, pairs, 0.0)
            pairs = pltpu.roll(pairs, rows + 1, 1, stride=1, stride_axis=0)
            lines.append(jnp.sum(pairs, axis=0, keepdims=True))
    taps = jnp.concatenate(lines, axis=0).astype(BF16)
    for peer in range(pay_ref.shape[0]):
        pay_ref[peer, :rows, :] = gated_ref[...]
        pay_ref[peer, rows:, :] = taps


def back_kernel(docs, per_group, where_ref, taps_ref, gate_ref, next_ref, k_ref, v_ref, key_ref, value_ref):
    rows, half = gate_ref.shape[0], 128
    mask = backward_mask(where_ref, docs, rows)
    ext = jnp.concatenate([gate_ref[...], next_ref[...]], axis=0)
    for side, total in enumerate(apply_bands(taps_ref, mask, ext, rows, half, per_group)):
        lanes = slice(side * half, (side + 1) * half)
        key_ref[:, lanes] = (total * v_ref[:, lanes].astype(F32)).astype(BF16)
        value_ref[:, lanes] = (total * k_ref[:, lanes].astype(F32)).astype(BF16)


def pick_kernel(unit, columns, rows_ref, out_ref):
    peers, part, wide = out_ref.shape
    block, lanes = rows_ref.shape[2], 128
    per_chunk, chunks = columns // unit, wide // columns
    low = iota((part, lanes), 1) < unit

    def half(index, upper):
        start = index * unit // lanes * lanes
        tile = rows_ref[start // block, :, start % block : start % block + lanes].astype(F32)
        return tile if (index % 2 == 1) == upper else pltpu.roll(tile, unit, 1)

    for peer in range(peers):
        units = [(c * peers + peer) * per_chunk + u for c in range(chunks) for u in range(per_chunk)]
        for tile in range(wide // lanes):
            a, b = units[2 * tile], units[2 * tile + 1]
            out_ref[peer, :, tile * lanes : (tile + 1) * lanes] = jnp.where(low, half(a, False), half(b, True)).astype(BF16)


def columns_to(docs, where_ref, n_zl, n_x, step, core, width):
    zl = lax.rem(where_ref[docs + 2] + step // n_x, n_zl)
    x = lax.rem(where_ref[docs + 3] + step % n_x, n_x)
    return pl.ds(pl.multiple_of(((zl * n_x + x) * 2 + core) * width, width), width)


def project_sent(docs, n_zl, n_x, where_ref, gated_ref, w_ref, out_ref):
    blocks, _, width = out_ref.shape
    core = 1 - where_ref[docs + 1]
    for step in range(blocks):
        lanes = columns_to(docs, where_ref, n_zl, n_x, step, core, width)
        out_ref[step] = jnp.dot(gated_ref[...], w_ref[:, lanes], preferred_element_type=F32).astype(BF16)


def project_kept(docs, n_zl, n_x, where_ref, gated_ref, w_ref, came_ref, *out_refs):
    blocks, _, width = came_ref.shape
    core = where_ref[docs + 1]
    for step in range(blocks):
        lanes = columns_to(docs, where_ref, n_zl, n_x, step, core, width)
        total = jnp.dot(gated_ref[...], w_ref[:, lanes], preferred_element_type=F32)
        out_refs[step % n_x][step // n_x] = (total + came_ref[step].astype(F32)).astype(BF16)


def call(kernel, outs, ins, scratch=(), name=None):
    ins = [a if a.dtype == jnp.int32 or name not in TIED else pltpu.with_memory_space_constraint(a, pltpu.VMEM) for a in ins]
    return pl.pallas_call(
        kernel,
        out_shape=outs,
        in_specs=[SMEM if a.dtype == jnp.int32 else VMEM for a in ins],
        out_specs=jax.tree.map(lambda _: VMEM, outs),
        scratch_shapes=list(scratch),
        compiler_params=pltpu.CompilerParams(vmem_limit_bytes=LIMITS.get(name, 16 << 20)),
    )(*ins)


def like(shape, dtype=BF16):
    return jax.ShapeDtypeStruct(shape, dtype)


def shifted(value, axis, steps):
    count = lax.axis_size(axis)
    leading, last = (max(0, -steps), min(count, count - steps))
    return lax.ppermute(value, axis, [(source, source + steps) for source in range(leading, last)])


def exchange(value, axes):
    return lax.all_to_all(value, axes, 0, 0, tiled=True)


def turned(value, axis, steps):
    count = lax.axis_size(axis)
    return lax.ppermute(value, axis, [(source, (source + steps) % count) for source in range(count)])


def swap_cores(value):
    return lax.ppermute(value, "core", [(0, 1), (1, 0)])


def block(query_in, key_in, value_in, filters, doc_lengths, w_out, cotangent):
    rows, width = query_in.shape
    groups, length = filters.shape
    part, per_group, docs = rows // 2, width // groups, doc_lengths.shape[0]
    n_zh, n_y, n_zl, n_x = (lax.axis_size(a) for a in ("zh", "y", "zl", "x"))
    n_chip = n_zl * n_x
    core, place = lax.axis_index("core"), lax.axis_index(SEQ)
    columns = n_chip * 2 * width // (n_zh * n_y)
    spots = jnp.stack([place * rows, core, lax.axis_index("zl"), lax.axis_index("x")])
    where = jnp.concatenate([doc_lengths, spots.astype(jnp.int32)])

    fan, product = call(
        entry_kernel, (like((2 * n_chip, part, width)), like((rows, width))), [cotangent, key_in, value_in], name="entry"
    )
    mine = exchange(fan, CHAN)
    prev = shifted(product, SEQ, 1)
    taps = filters.astype(F32)
    zeros = jnp.zeros((groups, 2 * rows - length), F32)
    ahead = jnp.concatenate([zeros[:, :1], jnp.flip(taps, 1), zeros[:, 1:]], axis=1)
    behind = jnp.concatenate([taps, zeros], axis=1)
    filtered, gated = call(
        lambda *r: filter_kernel(docs, per_group, *r), (like((rows, width), F32), like((rows, width))),
        [where, ahead, prev, product, query_in], name="filter",
    )
    mine, gated = lax.optimization_barrier((mine, gated))
    picked = call(lambda *r: pick_kernel(64, columns, *r), like((n_y, part, n_zh * columns)), [mine], name="pick")
    picked = exchange(picked, "y")
    sent = call(
        lambda *r: project_sent(docs, n_zl, n_x, *r), like((n_chip, rows, width)), [where, gated, w_out], name="sent"
    )
    other, came = swap_cores(mine), swap_cores(sent)
    parts = call(
        lambda *r: project_kept(docs, n_zl, n_x, *r), (like((n_zl, rows, width)),) * n_x,
        [where, gated, w_out, came], name="kept",
    )
    gate, grad_query, pay = call(
        lambda *r: grad_kernel(docs, per_group, *r),
        (like((rows, width)), like((rows, width)), like((n_y, rows + groups, width))),
        [where, mine, other, w_out, query_in, filtered, gated, prev, product],
        [pltpu.VMEM((rows, width), F32)], name="grad",
    )
    gathered = exchange(pay, "y")
    picked_other = swap_cores(picked)
    following = shifted(gate, SEQ, -1)
    grad_key, grad_value = call(
        lambda *r: back_kernel(docs, per_group, *r), (like((rows, width)), like((rows, width))),
        [where, behind, gate, following, key_in, value_in], name="back",
    )
    along_x = sum((turned(parts[k], "x", k).astype(F32) for k in range(1, n_x)), parts[0].astype(F32)).astype(BF16)
    gathered, grad_key, grad_value, along_x = lax.optimization_barrier((gathered, grad_key, grad_value, along_x))
    block_out = sum((turned(along_x[k], "zl", k).astype(F32) for k in range(1, n_zl)), along_x[0].astype(F32)).astype(BF16)

    upper, lower = gathered[:, :part], gathered[:, part:rows]
    weight = jnp.einsum("ytn,ytc->nc", picked, jnp.where(core == 0, upper, lower), preferred_element_type=F32)
    weight += jnp.einsum("ytn,ytc->nc", picked_other, jnp.where(core == 0, lower, upper), preferred_element_type=F32)
    tap_terms = jnp.sum(gathered[:, rows:].astype(F32), axis=0).astype(BF16)
    terms = jnp.concatenate(
        [weight.astype(BF16).reshape(n_zh, columns, width), jnp.broadcast_to(tap_terms[None], (n_zh, groups, width))], axis=1
    )
    total = jnp.sum(exchange(terms, "zh").astype(F32), axis=0)
    owned = length // (n_zh * n_y)
    tap_sum = lax.dynamic_slice_in_dim(total[columns:], rows + 1 - (place + 1) * owned, owned, 1)
    return (block_out, grad_query, grad_key, grad_value, total[:columns].T.astype(BF16), jnp.flip(tap_sum, 1))


def build(fine):
    both, rows = P(SEQ, CHAN), P(CHAN, None)
    return jax.shard_map(
        block,
        mesh=fine,
        in_specs=(both, both, both, rows, P(), rows, both),
        out_specs=(both, both, both, both, P(CHAN, SEQ), P(CHAN, SEQ)),
        check_vma=False,
    )


def solution(mesh):
    fine = Mesh(mesh.devices.reshape(4, 8, 3, 4, 2), SEQ + CHAN)
    return build(fine)
```
